256 devices in a mesh: wave: 8 (over z_hi, core), brick: 32 (over z_lo, x, y).
Axes of the slice: x: 4, y: 4, z: 8 (z_hi: 4, z_lo: 2; z = z_hi * 2 + z_lo), core: 2. Of those that a mesh axis runs over, the one named last changes fastest.
Arguments:
- sources: float32 [8, 6, 256, 6, 4096], P('wave', None, 'brick'), may hold values from -6 to 6
- permittivity: float32 [256, 6, 4096], P('brick'), may hold values from 1 to 4
- wave_number_sq: float32 [8], P('wave'), may hold values from 0.5 to 3
- pixel_list: int32 [32, 256], P('brick'), may hold values from 0 to 255, each once within a row
Outputs:
- design_grad: float32 [32, 32768], P('brick')
The draws below stay inside these ranges and needn't reach their ends.
Inputs may be any that keep to these rules, and one draw needn't show every extreme that they name: `pixel_list`: each row is a permutation of 0 to 255.
All inputs are finite; a program needn't handle non-finite values.
Results may differ from the reference program's by a relative error of at most 0.0001.
Values sent between devices are 32-bit elements; how exact they have to be, the bound alone decides.
A program may use at most 128 MiB of HBM per device.

```python
import math
import jax
import jax.numpy as jnp
from jax import lax

BX = 8
LZ = 6
NY = 4096
SWEEPS = 3
RADIUS = 2
RUN = 128
NX = 256
WAVES = 8
PIX_DEV = 32768
N_BRICK = 32


def shard_levels(stream_key, shape, pieces, smallest, largest):
    level, own = 1.0, jax.random.fold_in(stream_key, 6)
    for position, shards_of in pieces:
        steps = jnp.exp(jax.random.uniform(jax.random.fold_in(own, position), (shards_of,), jnp.float32, smallest / len(pieces), largest / len(pieces)))
        level = level * jnp.repeat(steps, shape[position] // shards_of).reshape([-1 if axis == position else 1 for axis in range(len(shape))])
    return level


def centred(rng, shape, scale, bound, pieces=(), kind=jnp.bfloat16):
    level = shard_levels(rng, shape, pieces, -0.22, 0.18) if pieces else 1.0
    values = jax.random.normal(rng, shape, jnp.float32) * scale * level
    return jnp.minimum(jnp.maximum(values, -bound), bound).astype(kind)


def setup_inputs(seed: int = 0) -> dict:
    key_of = jax.random.split(jax.random.key(seed), 5)
    sources = centred(key_of[0], (WAVES, 6, NX, LZ, NY), 1.0, 6.0, ((0, 8), (2, 32)), jnp.float32)
    permittivity = jnp.clip(1.0 + 3.0 * jax.random.uniform(key_of[1], (NX, LZ, NY), jnp.float32) ** shard_levels(key_of[1], (NX, LZ, NY), ((0, 32),), -0.2, 0.2), 1.0, 4.0)
    wave_number_sq = jnp.clip(jnp.exp(math.log(3.0) - 1.7917595 * jax.random.uniform(key_of[2], (WAVES,), jnp.float32) ** shard_levels(key_of[2], (WAVES,), ((0, 8),), -0.2, 0.2)), 0.5, 3.0)
    pixel_list = jax.vmap(lambda own: jax.random.permutation(own, PIX_DEV // RUN))(jax.random.split(key_of[3], N_BRICK)).reshape((N_BRICK, PIX_DEV // RUN)).astype(jnp.int32)
    return dict(sources=sources, permittivity=permittivity, wave_number_sq=wave_number_sq, pixel_list=pixel_list)


RELAX = 0.5


def ahead_x(values):
    return values[..., 1:, :, :] - values[..., :-1, :, :]


def ahead_y(values):
    return jnp.concatenate([values[..., 1:], jnp.zeros_like(values[..., :1])], -1) - values


def ahead_z(values):
    return jnp.concatenate([values[..., 1:, :], jnp.zeros_like(values[..., :1, :])], -2) - values


def behind_y(values):
    return values - jnp.concatenate([jnp.zeros_like(values[..., :1]), values[..., :-1]], -1)


def behind_z(values):
    return values - jnp.concatenate([jnp.zeros_like(values[..., :1, :]), values[..., :-1, :]], -2)


def curl_curl(padded):
    comp_x = padded[..., 0, :, :, :]
    comp_y = padded[..., 1, :, :, :]
    comp_z = padded[..., 2, :, :, :]
    lead_x = comp_x[..., :-1, :, :]
    lead_y = comp_y[..., :-1, :, :]
    lead_z = comp_z[..., :-1, :, :]
    mag_x = ahead_y(lead_z) - ahead_z(lead_y)
    mag_y = ahead_z(lead_x) - ahead_x(comp_z)
    mag_z = ahead_x(comp_y) - ahead_y(lead_x)
    curl_x = behind_y(mag_z[..., 1:, :, :]) - behind_z(mag_y[..., 1:, :, :])
    curl_y = behind_z(mag_x[..., 1:, :, :]) - ahead_x(mag_z)
    curl_z = ahead_x(mag_y) - behind_y(mag_x[..., 1:, :, :])
    return jnp.stack([curl_x, curl_y, curl_z], -4)


def relax_step(fields, padded, drive_all, permit, wave_sq, diagonal):
    return fields + RELAX * (drive_all - curl_curl(padded) - wave_sq * permit * fields) / diagonal


def smooth_padded(padded, length, along):
    summed = jnp.zeros_like(lax.slice_in_dim(padded, 0, length, axis=along))
    for offset in range(2 * RADIUS + 1):
        weight = (RADIUS + 1 - abs(offset - RADIUS)) / (RADIUS + 1) ** 2
        summed = summed + weight * lax.slice_in_dim(padded, offset, offset + length, axis=along)
    return summed


def reference(sources, permittivity, wave_number_sq, pixel_list):
    gradient = jnp.zeros((NX, NY), jnp.float32)
    for wave in range(WAVES):
        wave_sq = wave_number_sq[wave]
        drive_all = sources[wave].reshape(2, 3, NX, LZ, NY)
        diagonal = 4.0 + wave_sq * permittivity
        fields = RELAX * drive_all / diagonal
        for sweep_index in range(SWEEPS - 1):
            padded = jnp.pad(fields, ((0, 0), (0, 0), (1, 1), (0, 0), (0, 0)))
            fields = relax_step(fields, padded, drive_all, permittivity, wave_sq, diagonal)
        gradient = gradient + (-wave_sq) * jnp.sum(fields[0] * fields[1], axis=(0, 2))
    smooth = smooth_padded(jnp.pad(gradient, ((0, 0), (RADIUS, RADIUS))), NY, 1)
    smooth = smooth_padded(jnp.pad(smooth, ((RADIUS, RADIUS), (0, 0))), NX, 0)
    blocks = smooth.reshape(NX // BX, (BX * NY) // RUN, RUN)
    picked = jnp.take_along_axis(blocks, pixel_list.astype(jnp.int32)[:, :, None], axis=1)
    return picked.reshape(NX // BX, BX * NY)
```

```python
import functools

import jax
import jax.numpy as jnp
from jax import lax
from jax.experimental import pallas as pl
from jax.experimental.pallas import tpu as pltpu
from jax.sharding import PartitionSpec as P

RADIUS = 2
RUN = 128
LANES = 128
MESH = pl.DeviceIdType.MESH
WEIGHTS = [(RADIUS + 1 - abs(d)) / (RADIUS + 1) ** 2 for d in range(RADIUS + 1)]


def columns_of(start, count):
    return pl.ds(start * LANES, count * LANES)


def block_at(j):
    return pl.ds(pl.multiple_of(j * LANES, LANES), LANES)


def windows(blocks, chunks, lag):
    per = blocks // chunks
    starts = [max(per * c - lag, 0) for c in range(chunks)] + [blocks]
    return list(zip(starts[:-1], starts[1:]))


def body(
    n_wave, n_brick, blocks, layers, chunks,
    wave_ref, pixel_ref, src, eps, out_ref,
    drive, permit, ratio, first, carry,
    out_left, out_right, in_left, in_right,
    density, edge_top, edge_bottom, parts, from_left, from_right, rows, whole, runs,
    load_sem, halo_send, halo_recv, part_send, part_recv, edge_send, edge_recv, gather_send, gather_recv,
):
    wave = lax.axis_index("wave")
    brick = lax.axis_index("brick")
    after = lax.rem(brick + 1, n_brick)
    before = lax.rem(brick + n_brick - 1, n_brick)
    peers = [lax.rem(wave + p, n_wave) for p in range(n_wave)]
    owned = blocks // n_wave
    fields = 3 * layers

    loads = []
    per = blocks // chunks
    for c in range(chunks):
        at = columns_of(per * c, per)
        pair = (
            pltpu.make_async_copy(eps.at[:, :, at], permit.at[:, :, at], load_sem.at[0, c]),
            pltpu.make_async_copy(src.at[:, :, at], drive.at[:, :, at], load_sem.at[1, c]),
        )
        for copy in pair:
            copy.start()
        loads.append(pair)

    barrier = pltpu.get_barrier_semaphore()
    for p in range(n_wave):
        if p:
            pl.semaphore_signal(barrier, inc=1, device_id=(peers[p], brick), device_id_type=MESH)
        for side in (before, after):
            pl.semaphore_signal(barrier, inc=1, device_id=(peers[p], side), device_id_type=MESH)

    wave_sq = wave_ref[0]
    lane = lax.broadcasted_iota(jnp.int32, (8, LANES), 1)
    row = lax.broadcasted_iota(jnp.int32, (8, LANES), 0)
    first_lane, last_lane = lane == 0, lane == LANES - 1
    first_row, last_row = row == 0, row == 7
    edge = columns_of(blocks, 1)
    nothing = jnp.zeros((8, LANES), jnp.float32)
    for plane in range(2 * fields):
        drive[plane, :, edge] = nothing
        first[plane, :, edge] = nothing
    for z in range(layers):
        ratio[z, :, edge] = nothing
    whole[:, columns_of(0, 1)] = nothing
    whole[:, columns_of(blocks + 1, 1)] = nothing

    def ahead_lane(now, later):
        return jnp.where(last_lane, pltpu.roll(later, LANES - 1, 1), pltpu.roll(now, LANES - 1, 1))

    def initial(f, comp, z, at):
        return ratio[z, :, at] * drive[f * fields + comp * layers + z, :, at]

    def swept(f, comp, z, at):
        return first[f * fields + comp * layers + z, :, at]

    def pack(value, step, j):
        at, later = block_at(j), block_at(j + 1)
        for f in range(2):
            x_here = [value(f, 0, z, at) for z in range(layers)]
            for z in range(layers):
                ex, ey, ez = x_here[z], value(f, 1, z, at), value(f, 2, z, at)
                gy = ey + (ahead_lane(ex, value(f, 0, z, later)) - ex)
                gz = ez + (x_here[z + 1] - ex) if z + 1 < layers else ez - ex
                k = f * 2 * layers + z
                out_right[step, k : k + 1, at] = gy[7:8]
                out_right[step, k + layers : k + layers + 1, at] = gz[7:8]
                out_left[step, k : k + 1, at] = ey[0:1]
                out_left[step, k + layers : k + layers + 1, at] = ez[0:1]

    def sweep(value, step, j, emit):
        at, later = block_at(j), block_at(j + 1)
        e = {}

        def get(f, comp, z):
            if (f, comp, z) not in e:
                e[f, comp, z] = value(f, comp, z, at)
            return e[f, comp, z]

        def spread(ref, k):
            return jnp.broadcast_to(ref[step, k : k + 1, at], (8, LANES))

        below = [None, None]
        for z in range(layers):
            r = ratio[z, :, at]
            s = 0.5 + 4.0 * r
            fresh = []
            for f in range(2):
                ex, ey, ez = get(f, 0, z), get(f, 1, z), get(f, 2, z)
                k = f * 2 * layers + z
                ex_y = ahead_lane(ex, value(f, 0, z, later))
                ez_y = ahead_lane(ez, value(f, 2, z, later))
                ey_x = jnp.where(last_row, spread(in_right, k), pltpu.roll(ey, 7, 0))
                ez_x = jnp.where(last_row, spread(in_right, k + layers), pltpu.roll(ez, 7, 0))
                if z + 1 < layers:
                    hx = (ez_y - ez) - (get(f, 1, z + 1) - ey)
                    hy = (get(f, 0, z + 1) - ex) - (ez_x - ez)
                else:
                    hx = (ez_y - ez) + ey
                    hy = (ez - ex) - ez_x
                hz = (ey_x - ey) - (ex_y - ex)
                hx_roll, hz_roll = pltpu.roll(hx, 1, 1), pltpu.roll(hz, 1, 1)
                hx_y = jnp.where(first_lane, carry[0, f * layers + z], hx_roll)
                hz_y = jnp.where(first_lane, carry[1, f * layers + z], hz_roll)
                carry[0, f * layers + z] = hx_roll
                carry[1, f * layers + z] = hz_roll
                hz_x = jnp.where(first_row, ey - spread(in_left, k), pltpu.roll(hz, 1, 0))
                hy_x = jnp.where(first_row, spread(in_left, k + layers) - ez, pltpu.roll(hy, 1, 0))
                cx = (hz - hz_y) - (hy if z == 0 else hy - below[f][1])
                cy = (hx if z == 0 else hx - below[f][0]) - (hz - hz_x)
                cz = (hy - hy_x) - (hx - hx_y)
                below[f] = (hx, hy)
                base = f * fields + z
                fresh.append(
                    [
                        s * here + r * (drive[base + comp * layers, :, at] - curl)
                        for comp, (here, curl) in enumerate(((ex, cx), (ey, cy), (ez, cz)))
                    ]
                )
            emit(z, at, fresh)

    def over(start, stop, step_of):
        def turn(j, state):
            step_of(j)
            return state

        lax.fori_loop(start, stop, turn, 0)

    def halo_copies(step, c, span):
        at = columns_of(span[0], span[1] - span[0])
        return [
            pltpu.make_async_remote_copy(
                src_ref=source.at[step, :, at],
                dst_ref=target.at[step, :, at],
                send_sem=halo_send.at[step, side, c],
                recv_sem=halo_recv.at[step, side, c],
                device_id=(wave, device),
                device_id_type=MESH,
            )
            for side, source, target, device in (
                (0, out_right, in_left, after),
                (1, out_left, in_right, before),
            )
        ]

    spans = [windows(blocks, chunks, 1), windows(blocks, chunks, 2)]
    copies = [[halo_copies(step, c, spans[step][c]) for c in range(chunks)] for step in range(2)]

    def arrive(step, c):
        for copy in copies[step][c]:
            copy.wait_recv()
        lo, hi = spans[step][c]
        at = columns_of(lo, hi - lo)

        @pl.when(brick == 0)
        def _():
            in_left[step, :, at] = jnp.zeros((4 * layers, (hi - lo) * LANES), jnp.float32)

        @pl.when(brick == n_brick - 1)
        def _():
            in_right[step, :, at] = jnp.zeros((4 * layers, (hi - lo) * LANES), jnp.float32)

    def set_ratio(j):
        at = block_at(j)
        for z in range(layers):
            ratio[z, :, at] = 0.5 / (4.0 + wave_sq * permit[z, :, at])

    for c in range(chunks):
        for copy in loads[c]:
            copy.wait()
        over(per * c, per * (c + 1), set_ratio)
        over(*spans[0][c], functools.partial(pack, initial, 0))
        if c == 0:
            pl.semaphore_wait(barrier, 3 * n_wave - 1)
        for copy in copies[0][c]:
            copy.start()

    def keep(z, at, fresh):
        for f in range(2):
            for comp in range(3):
                first[f * fields + comp * layers + z, :, at] = fresh[f][comp]

    def sweep_first(j):
        sweep(initial, 0, j, keep)

    carry[...] = jnp.zeros_like(carry)
    for c in range(chunks):
        arrive(0, c)
        over(*spans[0][c], sweep_first)
        over(*spans[1][c], functools.partial(pack, swept, 1))
        for copy in copies[1][c]:
            copy.start()

    def sweep_second(j):
        total = []

        def add(z, at, fresh):
            product = sum(fresh[0][comp] * fresh[1][comp] for comp in range(3))
            total[:] = [product if z == 0 else total[0] + product]

        sweep(swept, 1, j, add)
        at = block_at(j)
        mine = -wave_sq * total[0]
        density[:, at] = mine
        owner, place = j // owned, lax.rem(j, owned) * 2
        edge_top[owner, pl.ds(place, 2), :] = mine[0:2]
        edge_bottom[owner, pl.ds(place, 2), :] = mine[6:8]

    carry[...] = jnp.zeros_like(carry)
    for c in range(chunks):
        arrive(1, c)
        over(*spans[1][c], sweep_second)

    def owner_columns(w):
        return pl.ds(pl.multiple_of(w * owned * LANES, LANES), owned * LANES)

    exchanges = []
    for p in range(n_wave):
        for side, source, target, device in (
            (0, edge_bottom, from_left, after),
            (1, edge_top, from_right, before),
        ):
            exchanges.append(
                pltpu.make_async_remote_copy(
                    src_ref=source.at[peers[p]],
                    dst_ref=target.at[p],
                    send_sem=edge_send.at[side, p],
                    recv_sem=edge_recv.at[side, p],
                    device_id=(peers[p], device),
                    device_id_type=MESH,
                )
            )
        if p:
            exchanges.append(
                pltpu.make_async_remote_copy(
                    src_ref=density.at[:, owner_columns(peers[p])],
                    dst_ref=parts.at[p - 1],
                    send_sem=part_send.at[p - 1],
                    recv_sem=part_recv.at[p - 1],
                    device_id=(peers[p], brick),
                    device_id_type=MESH,
                )
            )
    for copy in exchanges:
        copy.start()
    for copy in exchanges:
        copy.wait_recv()

    total = density[:, owner_columns(wave)]
    for p in range(n_wave - 1):
        total = total + parts[p]
    left, right = from_left[0], from_right[0]
    for p in range(1, n_wave):
        left = left + from_left[p]
        right = right + from_right[p]
    left = jnp.where(brick == 0, 0.0, left)
    right = jnp.where(brick == n_brick - 1, 0.0, right)
    rows[8:16, :] = total
    for k in range(owned):
        at = columns_of(k, 1)
        rows[6:8, at] = left[2 * k : 2 * k + 2]
        rows[16:18, at] = right[2 * k : 2 * k + 2]
    mixed = WEIGHTS[0] * rows[8:16, :]
    for d in (1, 2):
        mixed = mixed + WEIGHTS[d] * (rows[8 - d : 16 - d, :] + rows[8 + d : 16 + d, :])
    mine = pl.ds(pl.multiple_of((wave * owned + 1) * LANES, LANES), owned * LANES)
    whole[:, mine] = mixed

    gathers = [
        pltpu.make_async_remote_copy(
            src_ref=whole.at[:, mine],
            dst_ref=whole.at[:, mine],
            send_sem=gather_send.at[p - 1],
            recv_sem=gather_recv.at[p - 1],
            device_id=(peers[p], brick),
            device_id_type=MESH,
        )
        for p in range(1, n_wave)
    ]
    for copy in gathers:
        copy.start()
    for step in range(2):
        for c in range(chunks):
            for copy in copies[step][c]:
                copy.wait_send()
    for copy in exchanges:
        copy.wait_send()
    for p in range(1, n_wave):
        sender = lax.rem(wave + n_wave - p, n_wave)
        theirs = pl.ds(pl.multiple_of((sender * owned + 1) * LANES, LANES), owned * LANES)
        pltpu.make_async_remote_copy(
            src_ref=whole.at[:, theirs],
            dst_ref=whole.at[:, theirs],
            send_sem=gather_send.at[p - 1],
            recv_sem=gather_recv.at[p - 1],
            device_id=(peers[p], brick),
            device_id_type=MESH,
        ).wait_recv()

    def shifted(now, beside, d):
        if d > 0:
            return jnp.where(lane >= LANES - d, pltpu.roll(beside, LANES - d, 1), pltpu.roll(now, LANES - d, 1))
        return jnp.where(lane < -d, pltpu.roll(beside, -d, 1), pltpu.roll(now, -d, 1))

    for k in range(blocks):
        back, now, later = (whole[:, columns_of(k + d, 1)] for d in range(3))
        smooth = WEIGHTS[0] * now
        for d in (1, 2):
            smooth = smooth + WEIGHTS[d] * (shifted(now, later, d) + shifted(now, back, -d))
        runs[pl.ds(k, 8, stride=blocks), :] = smooth

    def pick(q, state):
        out_ref[pl.ds(q, 1), :] = runs[pl.ds(pixel_ref[0, q], 1), :]
        return state

    lax.fori_loop(0, 8 * blocks, pick, 0, unroll=16)
    for copy in gathers:
        copy.wait_send()


def on_device(n_wave, n_brick, chunks, sources, permittivity, wave_number_sq, pixel_list):
    rows, layers, length = permittivity.shape
    blocks = length // LANES
    owned = blocks // n_wave
    planes = 6 * layers
    src = sources[0].transpose(0, 2, 1, 3).reshape(planes, rows, length)
    eps = permittivity.transpose(1, 0, 2)
    vmem, dma, f32 = pltpu.VMEM, pltpu.SemaphoreType.DMA, jnp.float32
    padded = length + LANES
    picked = pl.pallas_call(
        functools.partial(body, n_wave, n_brick, blocks, layers, chunks),
        out_shape=jax.ShapeDtypeStruct((rows * blocks, RUN), f32),
        in_specs=[
            pl.BlockSpec(memory_space=pltpu.SMEM),
            pl.BlockSpec(memory_space=pltpu.SMEM),
            pl.BlockSpec(memory_space=pl.ANY),
            pl.BlockSpec(memory_space=pl.ANY),
        ],
        out_specs=pl.BlockSpec(memory_space=pltpu.VMEM),
        scratch_shapes=[
            vmem((planes, rows, padded), f32),
            vmem((layers, rows, length), f32),
            vmem((layers, rows, padded), f32),
            vmem((planes, rows, padded), f32),
            vmem((2, 2 * layers, rows, LANES), f32),
            vmem((2, 4 * layers, length), f32),
            vmem((2, 4 * layers, length), f32),
            vmem((2, 4 * layers, length), f32),
            vmem((2, 4 * layers, length), f32),
            vmem((rows, length), f32),
            vmem((n_wave, 2 * owned, LANES), f32),
            vmem((n_wave, 2 * owned, LANES), f32),
            vmem((n_wave - 1, rows, owned * LANES), f32),
            vmem((n_wave, 2 * owned, LANES), f32),
            vmem((n_wave, 2 * owned, LANES), f32),
            vmem((24, owned * LANES), f32),
            vmem((rows, length + 2 * LANES), f32),
            vmem((rows * blocks, RUN), f32),
            dma((2, chunks)),
            dma((2, 2, chunks)),
            dma((2, 2, chunks)),
            dma((n_wave - 1,)),
            dma((n_wave - 1,)),
            dma((2, n_wave)),
            dma((2, n_wave)),
            dma((n_wave - 1,)),
            dma((n_wave - 1,)),
        ],
        compiler_params=pltpu.CompilerParams(
            collective_id=0, has_side_effects=True, vmem_limit_bytes=60 * 1024 * 1024
        ),
    )(wave_number_sq, pixel_list, src, eps)
    return picked.reshape(1, rows * length)


def solution(mesh, chunks=4):
    n_wave, n_brick = mesh.shape["wave"], mesh.shape["brick"]
    return jax.shard_map(
        functools.partial(on_device, n_wave, n_brick, chunks),
        mesh=mesh,
        in_specs=(
            P("wave", None, "brick", None, None),
            P("brick", None, None),
            P("wave"),
            P("brick", None),
        ),
        out_specs=P("brick", None),
        check_vma=False,
    )
```

```python
import functools

import jax
import jax.numpy as jnp
from jax import lax
from jax.experimental import pallas as pl
from jax.experimental.pallas import tpu as pltpu
from jax.sharding import PartitionSpec as P

RADIUS = 2
RUN = 128
LANES = 128
MESH = pl.DeviceIdType.MESH
WEIGHTS = [(RADIUS + 1 - abs(d)) / (RADIUS + 1) ** 2 for d in range(RADIUS + 1)]


def columns_of(start, count):
    return pl.ds(start * LANES, count * LANES)


def block_at(j):
    return pl.ds(pl.multiple_of(j * LANES, LANES), LANES)


def windows(blocks, chunks, lag):
    per = blocks // chunks
    starts = [max(per * c - lag, 0) for c in range(chunks)] + [blocks]
    return list(zip(starts[:-1], starts[1:]))


def body(
    n_wave, n_brick, blocks, layers, chunks,
    wave_ref, pixel_ref, src, eps, out_ref,
    drive, permit, ratio, first, carry,
    out_left, out_right, in_left, in_right,
    density, edge_top, edge_bottom, parts, from_left, from_right, rows, whole, runs,
    load_sem, halo_send, halo_recv, part_send, part_recv, edge_send, edge_recv, gather_send, gather_recv,
):
    wave = lax.axis_index("wave")
    brick = lax.axis_index("brick")
    after = lax.rem(brick + 1, n_brick)
    before = lax.rem(brick + n_brick - 1, n_brick)
    peers = [lax.rem(wave + p, n_wave) for p in range(n_wave)]
    owned = blocks // n_wave
    fields = 3 * layers

    loads = []
    per = blocks // chunks
    for c in range(chunks):
        at = columns_of(per * c, per)
        pair = (
            pltpu.make_async_copy(eps.at[:, :, at], permit.at[:, :, at], load_sem.at[0, c]),
            pltpu.make_async_copy(src.at[:, :, at], drive.at[:, :, at], load_sem.at[1, c]),
        )
        for copy in pair:
            copy.start()
        loads.append(pair)

    barrier = pltpu.get_barrier_semaphore()
    for side in (before, after):
        pl.semaphore_signal(barrier, inc=1, device_id=(wave, side), device_id_type=MESH)
    for p in range(1, n_wave):
        pl.semaphore_signal(barrier, inc=1, device_id=(peers[p], brick), device_id_type=MESH)

    wave_sq = wave_ref[0]
    lane = lax.broadcasted_iota(jnp.int32, (8, LANES), 1)
    row = lax.broadcasted_iota(jnp.int32, (8, LANES), 0)
    first_lane, last_lane = lane == 0, lane == LANES - 1
    first_row, last_row = row == 0, row == 7
    edge = columns_of(blocks, 1)
    nothing = jnp.zeros((8, LANES), jnp.float32)
    for plane in range(2 * fields):
        drive[plane, :, edge] = nothing
        first[plane, :, edge] = nothing
    for z in range(layers):
        ratio[z, :, edge] = nothing
    whole[:, columns_of(0, 1)] = nothing
    whole[:, columns_of(blocks + 1, 1)] = nothing

    def ahead_lane(now, later):
        return jnp.where(last_lane, pltpu.roll(later, LANES - 1, 1), pltpu.roll(now, LANES - 1, 1))

    def initial(f, comp, z, at):
        return ratio[z, :, at] * drive[f * fields + comp * layers + z, :, at]

    def swept(f, comp, z, at):
        return first[f * fields + comp * layers + z, :, at]

    def pack(value, step, j):
        at, later = block_at(j), block_at(j + 1)
        for f in range(2):
            x_here = [value(f, 0, z, at) for z in range(layers)]
            for z in range(layers):
                ex, ey, ez = x_here[z], value(f, 1, z, at), value(f, 2, z, at)
                gy = ey + (ahead_lane(ex, value(f, 0, z, later)) - ex)
                gz = ez + (x_here[z + 1] - ex) if z + 1 < layers else ez - ex
                k = f * 2 * layers + z
                out_right[step, k : k + 1, at] = gy[7:8]
                out_right[step, k + layers : k + layers + 1, at] = gz[7:8]
                out_left[step, k : k + 1, at] = ey[0:1]
                out_left[step, k + layers : k + layers + 1, at] = ez[0:1]

    def sweep(value, step, j, emit):
        at, later = block_at(j), block_at(j + 1)
        e = {}

        def get(f, comp, z):
            if (f, comp, z) not in e:
                e[f, comp, z] = value(f, comp, z, at)
            return e[f, comp, z]

        def spread(ref, k):
            return jnp.broadcast_to(ref[step, k : k + 1, at], (8, LANES))

        below = [None, None]
        for z in range(layers):
            r = ratio[z, :, at]
            s = 0.5 + 4.0 * r
            fresh = []
            for f in range(2):
                ex, ey, ez = get(f, 0, z), get(f, 1, z), get(f, 2, z)
                k = f * 2 * layers + z
                ex_y = ahead_lane(ex, value(f, 0, z, later))
                ez_y = ahead_lane(ez, value(f, 2, z, later))
                ey_x = jnp.where(last_row, spread(in_right, k), pltpu.roll(ey, 7, 0))
                ez_x = jnp.where(last_row, spread(in_right, k + layers), pltpu.roll(ez, 7, 0))
                if z + 1 < layers:
                    hx = (ez_y - ez) - (get(f, 1, z + 1) - ey)
                    hy = (get(f, 0, z + 1) - ex) - (ez_x - ez)
                else:
                    hx = (ez_y - ez) + ey
                    hy = (ez - ex) - ez_x
                hz = (ey_x - ey) - (ex_y - ex)
                hx_roll, hz_roll = pltpu.roll(hx, 1, 1), pltpu.roll(hz, 1, 1)
                hx_y = jnp.where(first_lane, carry[0, f * layers + z], hx_roll)
                hz_y = jnp.where(first_lane, carry[1, f * layers + z], hz_roll)
                carry[0, f * layers + z] = hx_roll
                carry[1, f * layers + z] = hz_roll
                hz_x = jnp.where(first_row, ey - spread(in_left, k), pltpu.roll(hz, 1, 0))
                hy_x = jnp.where(first_row, spread(in_left, k + layers) - ez, pltpu.roll(hy, 1, 0))
                cx = (hz - hz_y) - (hy if z == 0 else hy - below[f][1])
                cy = (hx if z == 0 else hx - below[f][0]) - (hz - hz_x)
                cz = (hy - hy_x) - (hx - hx_y)
                below[f] = (hx, hy)
                base = f * fields + z
                fresh.append(
                    [
                        s * here + r * (drive[base + comp * layers, :, at] - curl)
                        for comp, (here, curl) in enumerate(((ex, cx), (ey, cy), (ez, cz)))
                    ]
                )
            emit(z, at, fresh)

    def over(start, stop, step_of):
        def turn(j, state):
            step_of(j)
            return state

        lax.fori_loop(start, stop, turn, 0)

    def halo_copies(step, c, span):
        at = columns_of(span[0], span[1] - span[0])
        return [
            pltpu.make_async_remote_copy(
                src_ref=source.at[step, :, at],
                dst_ref=target.at[step, :, at],
                send_sem=halo_send.at[step, side, c],
                recv_sem=halo_recv.at[step, side, c],
                device_id=(wave, device),
                device_id_type=MESH,
            )
            for side, source, target, device in (
                (0, out_right, in_left, after),
                (1, out_left, in_right, before),
            )
        ]

    spans = [windows(blocks, chunks, 1), windows(blocks, chunks, 2)]
    copies = [[halo_copies(step, c, spans[step][c]) for c in range(chunks)] for step in range(2)]

    def arrive(step, c):
        for copy in copies[step][c]:
            copy.wait_recv()
        lo, hi = spans[step][c]
        at = columns_of(lo, hi - lo)

        @pl.when(brick == 0)
        def _():
            in_left[step, :, at] = jnp.zeros((4 * layers, (hi - lo) * LANES), jnp.float32)

        @pl.when(brick == n_brick - 1)
        def _():
            in_right[step, :, at] = jnp.zeros((4 * layers, (hi - lo) * LANES), jnp.float32)

    def set_ratio(j):
        at = block_at(j)
        for z in range(layers):
            ratio[z, :, at] = 0.5 / (4.0 + wave_sq * permit[z, :, at])

    for c in range(chunks):
        for copy in loads[c]:
            copy.wait()
        over(per * c, per * (c + 1), set_ratio)
        over(*spans[0][c], functools.partial(pack, initial, 0))

    pl.semaphore_wait(barrier, n_wave + 1)
    for c in range(chunks):
        for copy in copies[0][c]:
            copy.start()

    def keep(z, at, fresh):
        for f in range(2):
            for comp in range(3):
                first[f * fields + comp * layers + z, :, at] = fresh[f][comp]

    def sweep_first(j):
        sweep(initial, 0, j, keep)

    carry[...] = jnp.zeros_like(carry)
    for c in range(chunks):
        arrive(0, c)
        over(*spans[0][c], sweep_first)
        over(*spans[1][c], functools.partial(pack, swept, 1))
        for copy in copies[1][c]:
            copy.start()

    def sweep_second(j):
        total = []

        def add(z, at, fresh):
            product = sum(fresh[0][comp] * fresh[1][comp] for comp in range(3))
            total[:] = [product if z == 0 else total[0] + product]

        sweep(swept, 1, j, add)
        at = block_at(j)
        mine = -wave_sq * total[0]
        density[:, at] = mine
        owner, place = j // owned, lax.rem(j, owned) * 2
        edge_top[owner, pl.ds(place, 2), :] = mine[0:2]
        edge_bottom[owner, pl.ds(place, 2), :] = mine[6:8]

    carry[...] = jnp.zeros_like(carry)
    for c in range(chunks):
        arrive(1, c)
        over(*spans[1][c], sweep_second)

    def owner_columns(w):
        return pl.ds(pl.multiple_of(w * owned * LANES, LANES), owned * LANES)

    exchanges = []
    for p in range(n_wave):
        for side, source, target, device in (
            (0, edge_bottom, from_left, after),
            (1, edge_top, from_right, before),
        ):
            exchanges.append(
                pltpu.make_async_remote_copy(
                    src_ref=source.at[peers[p]],
                    dst_ref=target.at[p],
                    send_sem=edge_send.at[side, p],
                    recv_sem=edge_recv.at[side, p],
                    device_id=(peers[p], device),
                    device_id_type=MESH,
                )
            )
        if p:
            exchanges.append(
                pltpu.make_async_remote_copy(
                    src_ref=density.at[:, owner_columns(peers[p])],
                    dst_ref=parts.at[p - 1],
                    send_sem=part_send.at[p - 1],
                    recv_sem=part_recv.at[p - 1],
                    device_id=(peers[p], brick),
                    device_id_type=MESH,
                )
            )
    for copy in exchanges:
        copy.start()
    for copy in exchanges:
        copy.wait_recv()

    total = density[:, owner_columns(wave)]
    for p in range(n_wave - 1):
        total = total + parts[p]
    left, right = from_left[0], from_right[0]
    for p in range(1, n_wave):
        left = left + from_left[p]
        right = right + from_right[p]
    left = jnp.where(brick == 0, 0.0, left)
    right = jnp.where(brick == n_brick - 1, 0.0, right)
    rows[8:16, :] = total
    for k in range(owned):
        at = columns_of(k, 1)
        rows[6:8, at] = left[2 * k : 2 * k + 2]
        rows[16:18, at] = right[2 * k : 2 * k + 2]
    mixed = WEIGHTS[0] * rows[8:16, :]
    for d in (1, 2):
        mixed = mixed + WEIGHTS[d] * (rows[8 - d : 16 - d, :] + rows[8 + d : 16 + d, :])
    mine = pl.ds(pl.multiple_of((wave * owned + 1) * LANES, LANES), owned * LANES)
    whole[:, mine] = mixed

    gathers = [
        pltpu.make_async_remote_copy(
            src_ref=whole.at[:, mine],
            dst_ref=whole.at[:, mine],
            send_sem=gather_send.at[p - 1],
            recv_sem=gather_recv.at[p - 1],
            device_id=(peers[p], brick),
            device_id_type=MESH,
        )
        for p in range(1, n_wave)
    ]
    for copy in gathers:
        copy.start()
    for step in range(2):
        for c in range(chunks):
            for copy in copies[step][c]:
                copy.wait_send()
    for copy in exchanges:
        copy.wait_send()
    for p in range(1, n_wave):
        sender = lax.rem(wave + n_wave - p, n_wave)
        theirs = pl.ds(pl.multiple_of((sender * owned + 1) * LANES, LANES), owned * LANES)
        pltpu.make_async_remote_copy(
            src_ref=whole.at[:, theirs],
            dst_ref=whole.at[:, theirs],
            send_sem=gather_send.at[p - 1],
            recv_sem=gather_recv.at[p - 1],
            device_id=(peers[p], brick),
            device_id_type=MESH,
        ).wait_recv()

    def shifted(now, beside, d):
        if d > 0:
            return jnp.where(lane >= LANES - d, pltpu.roll(beside, LANES - d, 1), pltpu.roll(now, LANES - d, 1))
        return jnp.where(lane < -d, pltpu.roll(beside, -d, 1), pltpu.roll(now, -d, 1))

    for k in range(blocks):
        back, now, later = (whole[:, columns_of(k + d, 1)] for d in range(3))
        smooth = WEIGHTS[0] * now
        for d in (1, 2):
            smooth = smooth + WEIGHTS[d] * (shifted(now, later, d) + shifted(now, back, -d))
        runs[pl.ds(k, 8, stride=blocks), :] = smooth

    def pick(q, state):
        out_ref[pl.ds(q, 1), :] = runs[pl.ds(pixel_ref[0, q], 1), :]
        return state

    lax.fori_loop(0, 8 * blocks, pick, 0, unroll=16)
    for copy in gathers:
        copy.wait_send()


def on_device(n_wave, n_brick, chunks, sources, permittivity, wave_number_sq, pixel_list):
    rows, layers, length = permittivity.shape
    blocks = length // LANES
    owned = blocks // n_wave
    planes = 6 * layers
    src = sources[0].transpose(0, 2, 1, 3).reshape(planes, rows, length)
    eps = permittivity.transpose(1, 0, 2)
    vmem, dma, f32 = pltpu.VMEM, pltpu.SemaphoreType.DMA, jnp.float32
    padded = length + LANES
    picked = pl.pallas_call(
        functools.partial(body, n_wave, n_brick, blocks, layers, chunks),
        out_shape=jax.ShapeDtypeStruct((rows * blocks, RUN), f32),
        in_specs=[
            pl.BlockSpec(memory_space=pltpu.SMEM),
            pl.BlockSpec(memory_space=pltpu.SMEM),
            pl.BlockSpec(memory_space=pl.ANY),
            pl.BlockSpec(memory_space=pl.ANY),
        ],
        out_specs=pl.BlockSpec(memory_space=pltpu.VMEM),
        scratch_shapes=[
            vmem((planes, rows, padded), f32),
            vmem((layers, rows, length), f32),
            vmem((layers, rows, padded), f32),
            vmem((planes, rows, padded), f32),
            vmem((2, 2 * layers, rows, LANES), f32),
            vmem((2, 4 * layers, length), f32),
            vmem((2, 4 * layers, length), f32),
            vmem((2, 4 * layers, length), f32),
            vmem((2, 4 * layers, length), f32),
            vmem((rows, length), f32),
            vmem((n_wave, 2 * owned, LANES), f32),
            vmem((n_wave, 2 * owned, LANES), f32),
            vmem((n_wave - 1, rows, owned * LANES), f32),
            vmem((n_wave, 2 * owned, LANES), f32),
            vmem((n_wave, 2 * owned, LANES), f32),
            vmem((24, owned * LANES), f32),
            vmem((rows, length + 2 * LANES), f32),
            vmem((rows * blocks, RUN), f32),
            dma((2, chunks)),
            dma((2, 2, chunks)),
            dma((2, 2, chunks)),
            dma((n_wave - 1,)),
            dma((n_wave - 1,)),
            dma((2, n_wave)),
            dma((2, n_wave)),
            dma((n_wave - 1,)),
            dma((n_wave - 1,)),
        ],
        compiler_params=pltpu.CompilerParams(
            collective_id=0, has_side_effects=True, vmem_limit_bytes=60 * 1024 * 1024
        ),
    )(wave_number_sq, pixel_list, src, eps)
    return picked.reshape(1, rows * length)


def solution(mesh, chunks=4):
    n_wave, n_brick = mesh.shape["wave"], mesh.shape["brick"]
    return jax.shard_map(
        functools.partial(on_device, n_wave, n_brick, chunks),
        mesh=mesh,
        in_specs=(
            P("wave", None, "brick", None, None),
            P("brick", None, None),
            P("wave"),
            P("brick", None),
        ),
        out_specs=P("brick", None),
        check_vma=False,
    )
```

```python
import functools

import jax
import jax.numpy as jnp
from jax import lax
from jax.experimental import pallas as pl
from jax.experimental.pallas import tpu as pltpu
from jax.sharding import PartitionSpec as P

RADIUS = 2
RUN = 128
LANES = 128
MESH = pl.DeviceIdType.MESH
WEIGHTS = [(RADIUS + 1 - abs(d)) / (RADIUS + 1) ** 2 for d in range(RADIUS + 1)]


def columns_of(start, count):
    return pl.ds(start * LANES, count * LANES)


def block_at(j):
    return pl.ds(pl.multiple_of(j * LANES, LANES), LANES)


def windows(blocks, chunks, lag):
    per = blocks // chunks
    starts = [max(per * c - lag, 0) for c in range(chunks)] + [blocks]
    return list(zip(starts[:-1], starts[1:]))


def body(
    n_wave, n_brick, blocks, layers, chunks,
    wave_ref, pixel_ref, src, eps, out_ref,
    drive, permit, ratio, first, carry,
    out_left, out_right, in_left, in_right,
    density, edge_top, edge_bottom, parts, from_left, from_right, rows, whole, runs,
    load_sem, halo_send, halo_recv, part_send, part_recv, edge_send, edge_recv, gather_send, gather_recv,
):
    wave = lax.axis_index("wave")
    brick = lax.axis_index("brick")
    after = lax.rem(brick + 1, n_brick)
    before = lax.rem(brick + n_brick - 1, n_brick)
    peers = [lax.rem(wave + p, n_wave) for p in range(n_wave)]
    owned = blocks // n_wave
    fields = 3 * layers

    loads = []
    per = blocks // chunks
    for c in range(chunks):
        at = columns_of(per * c, per)
        pair = (
            pltpu.make_async_copy(eps.at[:, :, at], permit.at[:, :, at], load_sem.at[0, c]),
            pltpu.make_async_copy(src.at[:, :, at], drive.at[:, :, at], load_sem.at[1, c]),
        )
        for copy in pair:
            copy.start()
        loads.append(pair)

    barrier = pltpu.get_barrier_semaphore()
    for side in (before, after):
        pl.semaphore_signal(barrier, inc=1, device_id=(wave, side), device_id_type=MESH)
    for p in range(1, n_wave):
        pl.semaphore_signal(barrier, inc=1, device_id=(peers[p], brick), device_id_type=MESH)

    wave_sq = wave_ref[0]
    lane = lax.broadcasted_iota(jnp.int32, (8, LANES), 1)
    row = lax.broadcasted_iota(jnp.int32, (8, LANES), 0)
    first_lane, last_lane = lane == 0, lane == LANES - 1
    first_row, last_row = row == 0, row == 7
    edge = columns_of(blocks, 1)
    nothing = jnp.zeros((8, LANES), jnp.float32)
    for plane in range(2 * fields):
        drive[plane, :, edge] = nothing
        first[plane, :, edge] = nothing
    for z in range(layers):
        ratio[z, :, edge] = nothing
    whole[:, columns_of(0, 1)] = nothing
    whole[:, columns_of(blocks + 1, 1)] = nothing

    def ahead_lane(now, later):
        return jnp.where(last_lane, pltpu.roll(later, LANES - 1, 1), pltpu.roll(now, LANES - 1, 1))

    def initial(f, comp, z, at):
        return ratio[z, :, at] * drive[f * fields + comp * layers + z, :, at]

    def swept(f, comp, z, at):
        return first[f * fields + comp * layers + z, :, at]

    def pack(value, step, j):
        at, later = block_at(j), block_at(j + 1)
        for f in range(2):
            x_here = [value(f, 0, z, at) for z in range(layers)]
            for z in range(layers):
                ex, ey, ez = x_here[z], value(f, 1, z, at), value(f, 2, z, at)
                gy = ey + (ahead_lane(ex, value(f, 0, z, later)) - ex)
                gz = ez + (x_here[z + 1] - ex) if z + 1 < layers else ez - ex
                k = f * 2 * layers + z
                out_right[step, k : k + 1, at] = gy[7:8]
                out_right[step, k + layers : k + layers + 1, at] = gz[7:8]
                out_left[step, k : k + 1, at] = ey[0:1]
                out_left[step, k + layers : k + layers + 1, at] = ez[0:1]

    def sweep(value, step, j, emit):
        at, later = block_at(j), block_at(j + 1)
        e = {}

        def get(f, comp, z):
            if (f, comp, z) not in e:
                e[f, comp, z] = value(f, comp, z, at)
            return e[f, comp, z]

        def spread(ref, k):
            return jnp.broadcast_to(ref[step, k : k + 1, at], (8, LANES))

        below = [None, None]
        for z in range(layers):
            r = ratio[z, :, at]
            s = 0.5 + 4.0 * r
            fresh = []
            for f in range(2):
                ex, ey, ez = get(f, 0, z), get(f, 1, z), get(f, 2, z)
                k = f * 2 * layers + z
                ex_y = ahead_lane(ex, value(f, 0, z, later))
                ez_y = ahead_lane(ez, value(f, 2, z, later))
                ey_x = jnp.where(last_row, spread(in_right, k), pltpu.roll(ey, 7, 0))
                ez_x = jnp.where(last_row, spread(in_right, k + layers), pltpu.roll(ez, 7, 0))
                if z + 1 < layers:
                    hx = (ez_y - ez) - (get(f, 1, z + 1) - ey)
                    hy = (get(f, 0, z + 1) - ex) - (ez_x - ez)
                else:
                    hx = (ez_y - ez) + ey
                    hy = (ez - ex) - ez_x
                hz = (ey_x - ey) - (ex_y - ex)
                hx_roll, hz_roll = pltpu.roll(hx, 1, 1), pltpu.roll(hz, 1, 1)
                hx_y = jnp.where(first_lane, carry[0, f * layers + z], hx_roll)
                hz_y = jnp.where(first_lane, carry[1, f * layers + z], hz_roll)
                carry[0, f * layers + z] = hx_roll
                carry[1, f * layers + z] = hz_roll
                hz_x = jnp.where(first_row, ey - spread(in_left, k), pltpu.roll(hz, 1, 0))
                hy_x = jnp.where(first_row, spread(in_left, k + layers) - ez, pltpu.roll(hy, 1, 0))
                cx = (hz - hz_y) - (hy if z == 0 else hy - below[f][1])
                cy = (hx if z == 0 else hx - below[f][0]) - (hz - hz_x)
                cz = (hy - hy_x) - (hx - hx_y)
                below[f] = (hx, hy)
                base = f * fields + z
                fresh.append(
                    [
                        s * here + r * (drive[base + comp * layers, :, at] - curl)
                        for comp, (here, curl) in enumerate(((ex, cx), (ey, cy), (ez, cz)))
                    ]
                )
            emit(z, at, fresh)

    def over(start, stop, step_of, unit=1):
        turns = (stop - start) // unit

        def turn(i, state):
            for k in range(unit):
                step_of(start + unit * i + k)
            return state

        lax.fori_loop(0, turns, turn, 0)
        if unit * turns < stop - start:
            over(start + unit * turns, stop, step_of)

    def halo_copies(step, c, span):
        at = columns_of(span[0], span[1] - span[0])
        return [
            pltpu.make_async_remote_copy(
                src_ref=source.at[step, :, at],
                dst_ref=target.at[step, :, at],
                send_sem=halo_send.at[step, side, c],
                recv_sem=halo_recv.at[step, side, c],
                device_id=(wave, device),
                device_id_type=MESH,
            )
            for side, source, target, device in (
                (0, out_right, in_left, after),
                (1, out_left, in_right, before),
            )
        ]

    spans = [windows(blocks, chunks, 1), windows(blocks, chunks, 2)]
    copies = [[halo_copies(step, c, spans[step][c]) for c in range(chunks)] for step in range(2)]

    def arrive(step, c):
        for copy in copies[step][c]:
            copy.wait_recv()
        lo, hi = spans[step][c]
        at = columns_of(lo, hi - lo)

        @pl.when(brick == 0)
        def _():
            in_left[step, :, at] = jnp.zeros((4 * layers, (hi - lo) * LANES), jnp.float32)

        @pl.when(brick == n_brick - 1)
        def _():
            in_right[step, :, at] = jnp.zeros((4 * layers, (hi - lo) * LANES), jnp.float32)

    def set_ratio(j):
        at = block_at(j)
        for z in range(layers):
            ratio[z, :, at] = 0.5 / (4.0 + wave_sq * permit[z, :, at])

    for c in range(chunks):
        for copy in loads[c]:
            copy.wait()
        over(per * c, per * (c + 1), set_ratio)
        over(*spans[0][c], functools.partial(pack, initial, 0), 2)
        if c == 0:
            pl.semaphore_wait(barrier, n_wave + 1)
        for copy in copies[0][c]:
            copy.start()

    def keep(z, at, fresh):
        for f in range(2):
            for comp in range(3):
                first[f * fields + comp * layers + z, :, at] = fresh[f][comp]

    def sweep_first(j):
        sweep(initial, 0, j, keep)

    carry[...] = jnp.zeros_like(carry)
    for c in range(chunks):
        arrive(0, c)
        over(*spans[0][c], sweep_first, 2)
        over(*spans[1][c], functools.partial(pack, swept, 1), 2)
        for copy in copies[1][c]:
            copy.start()

    def sweep_second(j):
        total = []

        def add(z, at, fresh):
            product = sum(fresh[0][comp] * fresh[1][comp] for comp in range(3))
            total[:] = [product if z == 0 else total[0] + product]

        sweep(swept, 1, j, add)
        at = block_at(j)
        mine = -wave_sq * total[0]
        density[:, at] = mine
        edge_top[j] = mine[0:2]
        edge_bottom[j] = mine[6:8]

    def exchange(g):
        made = []
        for p in range(n_wave):
            b = n_wave * g + peers[p]
            for side, source, target, device in (
                (0, edge_bottom, from_left, after),
                (1, edge_top, from_right, before),
            ):
                made.append(
                    pltpu.make_async_remote_copy(
                        src_ref=source.at[b],
                        dst_ref=target.at[g, p],
                        send_sem=edge_send.at[side, g, p],
                        recv_sem=edge_recv.at[side, g, p],
                        device_id=(peers[p], device),
                        device_id_type=MESH,
                    )
                )
            if p:
                made.append(
                    pltpu.make_async_remote_copy(
                        src_ref=density.at[:, block_at(b)],
                        dst_ref=parts.at[g, p - 1],
                        send_sem=part_send.at[g, p - 1],
                        recv_sem=part_recv.at[g, p - 1],
                        device_id=(peers[p], brick),
                        device_id_type=MESH,
                    )
                )
        return made

    def gather(g, owner):
        at = block_at(n_wave * g + owner + 1)
        return [
            pltpu.make_async_remote_copy(
                src_ref=whole.at[:, at],
                dst_ref=whole.at[:, at],
                send_sem=gather_send.at[g, p - 1],
                recv_sem=gather_recv.at[g, p - 1],
                device_id=(peers[p], brick),
                device_id_type=MESH,
            )
            for p in range(1, n_wave)
        ]

    exchanges = [exchange(g) for g in range(owned)]
    gathers = [gather(g, wave) for g in range(owned)]

    def finish(g):
        for copy in exchanges[g]:
            copy.wait_recv()
        total = density[:, block_at(n_wave * g + wave)]
        for p in range(n_wave - 1):
            total = total + parts[g, p]
        left, right = from_left[g, 0], from_right[g, 0]
        for p in range(1, n_wave):
            left = left + from_left[g, p]
            right = right + from_right[g, p]
        rows[8:16, :] = total
        rows[6:8, :] = jnp.where(brick == 0, 0.0, left)
        rows[16:18, :] = jnp.where(brick == n_brick - 1, 0.0, right)
        mixed = WEIGHTS[0] * rows[8:16, :]
        for d in (1, 2):
            mixed = mixed + WEIGHTS[d] * (rows[8 - d : 16 - d, :] + rows[8 + d : 16 + d, :])
        whole[:, block_at(n_wave * g + wave + 1)] = mixed
        for copy in gathers[g]:
            copy.start()

    carry[...] = jnp.zeros_like(carry)
    begun = done = 0
    for c in range(chunks):
        arrive(1, c)
        over(*spans[1][c], sweep_second, 2)
        while begun < owned and spans[1][c][1] >= n_wave * (begun + 1):
            for copy in exchanges[begun]:
                copy.start()
            begun += 1
        if c >= chunks - 2 and done < begun - 2:
            finish(done)
            done += 1
    for g in range(done, owned):
        finish(g)

    for step in range(2):
        for c in range(chunks):
            for copy in copies[step][c]:
                copy.wait_send()
    for g in range(owned):
        for copy in exchanges[g]:
            copy.wait_send()
    for g in range(owned):
        for p in range(1, n_wave):
            sender = lax.rem(wave + n_wave - p, n_wave)
            gather(g, sender)[p - 1].wait_recv()

    def shifted(now, beside, d):
        if d > 0:
            return jnp.where(lane >= LANES - d, pltpu.roll(beside, LANES - d, 1), pltpu.roll(now, LANES - d, 1))
        return jnp.where(lane < -d, pltpu.roll(beside, -d, 1), pltpu.roll(now, -d, 1))

    for k in range(blocks):
        back, now, later = (whole[:, columns_of(k + d, 1)] for d in range(3))
        smooth = WEIGHTS[0] * now
        for d in (1, 2):
            smooth = smooth + WEIGHTS[d] * (shifted(now, later, d) + shifted(now, back, -d))
        runs[pl.ds(k, 8, stride=blocks), :] = smooth

    def pick(q, state):
        out_ref[pl.ds(q, 1), :] = runs[pl.ds(pixel_ref[0, q], 1), :]
        return state

    lax.fori_loop(0, 8 * blocks, pick, 0, unroll=16)
    for g in range(owned):
        for copy in gathers[g]:
            copy.wait_send()


def on_device(n_wave, n_brick, chunks, sources, permittivity, wave_number_sq, pixel_list):
    rows, layers, length = permittivity.shape
    blocks = length // LANES
    owned = blocks // n_wave
    planes = 6 * layers
    src = sources[0].transpose(0, 2, 1, 3).reshape(planes, rows, length)
    eps = permittivity.transpose(1, 0, 2)
    vmem, dma, f32 = pltpu.VMEM, pltpu.SemaphoreType.DMA, jnp.float32
    padded = length + LANES
    picked = pl.pallas_call(
        functools.partial(body, n_wave, n_brick, blocks, layers, chunks),
        out_shape=jax.ShapeDtypeStruct((rows * blocks, RUN), f32),
        in_specs=[
            pl.BlockSpec(memory_space=pltpu.SMEM),
            pl.BlockSpec(memory_space=pltpu.SMEM),
            pl.BlockSpec(memory_space=pl.ANY),
            pl.BlockSpec(memory_space=pl.ANY),
        ],
        out_specs=pl.BlockSpec(memory_space=pltpu.VMEM),
        scratch_shapes=[
            vmem((planes, rows, padded), f32),
            vmem((layers, rows, length), f32),
            vmem((layers, rows, padded), f32),
            vmem((planes, rows, padded), f32),
            vmem((2, 2 * layers, rows, LANES), f32),
            vmem((2, 4 * layers, length), f32),
            vmem((2, 4 * layers, length), f32),
            vmem((2, 4 * layers, length), f32),
            vmem((2, 4 * layers, length), f32),
            vmem((rows, length), f32),
            vmem((blocks, 2, LANES), f32),
            vmem((blocks, 2, LANES), f32),
            vmem((owned, n_wave - 1, rows, LANES), f32),
            vmem((owned, n_wave, 2, LANES), f32),
            vmem((owned, n_wave, 2, LANES), f32),
            vmem((24, LANES), f32),
            vmem((rows, length + 2 * LANES), f32),
            vmem((rows * blocks, RUN), f32),
            dma((2, chunks)),
            dma((2, 2, chunks)),
            dma((2, 2, chunks)),
            dma((owned, n_wave - 1)),
            dma((owned, n_wave - 1)),
            dma((2, owned, n_wave)),
            dma((2, owned, n_wave)),
            dma((owned, n_wave - 1)),
            dma((owned, n_wave - 1)),
        ],
        compiler_params=pltpu.CompilerParams(
            collective_id=0, has_side_effects=True, vmem_limit_bytes=60 * 1024 * 1024
        ),
    )(wave_number_sq, pixel_list, src, eps)
    return picked.reshape(1, rows * length)


def solution(mesh, chunks=4):
    n_wave, n_brick = mesh.shape["wave"], mesh.shape["brick"]
    return jax.shard_map(
        functools.partial(on_device, n_wave, n_brick, chunks),
        mesh=mesh,
        in_specs=(
            P("wave", None, "brick", None, None),
            P("brick", None, None),
            P("wave"),
            P("brick", None),
        ),
        out_specs=P("brick", None),
        check_vma=False,
    )
```
